32 devices in a mesh: src: 4 (over y, core), dst: 8 (over z, x).
Axes of the slice: x: 2, y: 2, z: 4, core: 2. Of those that a mesh axis runs over, the one named last changes fastest.
Arguments:
- features: bfloat16 [8192, 768], P(('src', 'dst')), may hold values from -6 to 6
- edge_tiles: bfloat16 [4, 8, 64, 128, 128], P('src', 'dst'), may hold values from -0.3125 to 0.3125
- tile_src: int32 [4, 8, 64], P('src', 'dst'), may hold values from 0 to 7
- tile_dst: int32 [4, 8, 64], P('src', 'dst'), may hold values from 0 to 15, as said below
- tile_count: int32 [4, 8], P('src', 'dst'), may hold values from 1 to 64, as said below
- weight: bfloat16 [768, 1024], replicated, may hold values from -0.21875 to 0.21875
- out_bias: float32 [1024], replicated, may hold values from -3 to 3
- out_grad: bfloat16 [8192, 1024], P(('src', 'dst')), may hold values from -6 to 6
Outputs:
- hidden: bfloat16 [8192, 1024], P(('src', 'dst'))
- feature_grad: bfloat16 [8192, 768], P(('src', 'dst'))
- weight_grad: float32 [768, 1024], replicated
- bias_grad: float32 [1024], replicated
The draws below stay inside these ranges and needn't reach their ends.
Inputs may be any that keep to these rules, and one draw needn't show every extreme that they name: `tile_src`: block s of the source column of device (i, k) is block s % 2 of device (s // 2, k). `tile_dst`: block e of the destination row of device (i, k) is block e % 2 of device (i, e // 2). On one device, all tile slots whose destination blocks lie on one device name the same block. In every row of devices, slot 0 of every device names one common block. `tile_count`: some device uses all 64 slots.
All inputs are finite; a program needn't handle non-finite values.
Results may differ from the reference program's by a relative error of at most 0.024.
Values may be sent and summed in bfloat16 or wider, within the bound.
A program may use at most 128 MiB of HBM per device.

```python
import jax
import jax.numpy as jnp
from jax import lax

F = 768
H = 1024
TILE = 128
BLK_DEV = 2
TILE_CAP = 64
NODES = 8192
N_SRC = 4
N_DST = 8


def draw_tile_dst(key, part):
    keys = jax.random.split(jax.random.fold_in(key, 7), 5)
    hub_master = jax.random.randint(keys[0], (N_SRC,), 0, N_DST)
    hub_block = jax.random.randint(keys[1], (N_SRC,), 0, BLK_DEV)
    table = jax.random.randint(keys[2], (N_SRC, N_DST, N_DST), 0, BLK_DEV)
    is_hub = jnp.arange(N_DST)[None, None, :] == hub_master[:, None, None]
    table = jnp.where(is_hub, hub_block[:, None, None], table)
    toward_hub = jax.random.randint(keys[3], (N_SRC, N_DST, TILE_CAP), 0, 2)
    others = jax.random.randint(keys[4], (N_SRC, N_DST, TILE_CAP), 0, N_DST)
    master = jnp.where(toward_hub == 1, hub_master[:, None, None], others)
    master = master.at[:, :, 0].set(jnp.broadcast_to(hub_master[:, None], (N_SRC, N_DST)))
    chosen = jnp.take_along_axis(table, master, axis=2)
    return (master * BLK_DEV + chosen).astype(jnp.int32)


def draw_tile_count(key, part):
    keys = jax.random.split(jax.random.fold_in(key, 11), 4)
    base_count = jax.random.randint(keys[0], (N_SRC, N_DST), 1, max(2, TILE_CAP // 2))
    heavy = jax.random.randint(keys[1], (N_SRC, N_DST), 0, 8) == 0
    large_count = jax.random.randint(keys[2], (N_SRC, N_DST), TILE_CAP // 2, TILE_CAP + 1)
    counts = jnp.where(heavy, large_count, base_count).reshape(N_SRC * N_DST)
    chosen_spot = jax.random.randint(keys[3], (), 0, N_SRC * N_DST)
    counts = counts.at[chosen_spot].set(TILE_CAP)
    return counts.reshape(N_SRC, N_DST).astype(jnp.int32)


def set_ends(values, rng, least, largest):
    index_at = [jax.random.randint(jax.random.fold_in(rng, axis), (), 0, length) for axis, length in enumerate(values.shape)]
    main_axis = values.shape.index(max(values.shape))
    beside = index_at[:main_axis] + [(index_at[main_axis] + 1) % values.shape[main_axis]] + index_at[main_axis + 1:]
    return values.at[tuple(index_at)].set(least).at[tuple(beside)].set(largest)


def raised(result, stream_key, source, target, parts, factor):
    def block_of(dim):
        return (jnp.arange(result.shape[dim]) // (result.shape[dim] // parts)).reshape((-1,) + (1,) * (result.ndim - 1 - dim))

    one_side = jax.random.permutation(stream_key, parts)[block_of(target)]
    other_side = (block_of(target) + parts // 2) % parts
    return jnp.where((block_of(source) == one_side) | (block_of(source) == other_side), factor * result, result)


def block_levels(stream_key, shape, shards, low, high):
    gain = 1.0
    for position, blocks in shards:
        heights = jax.random.uniform(jax.random.fold_in(jax.random.fold_in(stream_key, 6), position), (blocks,), jnp.float32, low / len(shards), high / len(shards))
        gain = gain * jnp.repeat(jnp.exp(heights), shape[position] // blocks).reshape((-1,) + (1,) * (len(shape) - 1 - position))
    return gain


def gaussian(own_key, dims, width, most, shards=(), kind=jnp.bfloat16):
    drawn = jax.random.normal(own_key, dims, jnp.float32) * width
    if len(shards) > 0:
        drawn = block_levels(own_key, dims, shards, -0.22, 0.18) * drawn
    return jnp.clip(drawn, min=-most, max=most).astype(kind)


def bell_draw_with(own_key, shape, width, bound, cuts, heavy, kind=jnp.bfloat16):
    entries = width * jax.random.normal(own_key, shape, jnp.float32)
    if cuts:
        entries = entries * block_levels(own_key, shape, cuts, -0.22, 0.18)
    return jnp.clip(raised(entries, jax.random.fold_in(own_key, 3), *heavy), -bound, bound).astype(kind)


def setup_inputs(seed: int = 0) -> dict:
    streams_of = jax.random.split(jax.random.key(seed), 9)
    return {
        "features": gaussian(streams_of[0], (NODES, F), 1.0, 6.0, ((0, 32),)),
        "edge_tiles": gaussian(streams_of[1], (N_SRC, N_DST, TILE_CAP, TILE, TILE), (3 * TILE) ** -0.5, 0.3125, ((0, 4), (1, 8))),
        "tile_src": set_ends(jax.random.randint(streams_of[2], (N_SRC, N_DST, TILE_CAP), 0, N_SRC * BLK_DEV), jax.random.fold_in(streams_of[2], 1), 0, (N_SRC * BLK_DEV) - 1).astype(jnp.int32),
        "tile_dst": draw_tile_dst(jax.random.fold_in(streams_of[8], 71), 0),
        "tile_count": draw_tile_count(jax.random.fold_in(streams_of[8], 71), 0),
        "weight": gaussian(streams_of[5], (F, H), F ** -0.5, 0.21875),
        "out_bias": gaussian(streams_of[6], (H,), 0.5, 3.0, (), jnp.float32),
        "out_grad": bell_draw_with(streams_of[7], (NODES, H), 1.0, 6.0, ((0, 32),), (0, 1, 32, 2.75)),
    }


def reference(features, edge_tiles, tile_src, tile_dst, tile_count, weight, out_bias, out_grad):
    capacity = edge_tiles.shape[2]
    col_blocks = N_SRC * BLK_DEV
    row_blocks = N_DST * BLK_DEV
    blocked = features.reshape(N_SRC, N_DST, BLK_DEV, TILE, F)
    slot_ids = jnp.arange(capacity, dtype=jnp.int32)
    device_ids = jnp.arange(N_SRC * N_DST, dtype=jnp.int32)

    def forward_step(aggregate, device_index):
        src_index = device_index // N_DST
        dst_index = device_index % N_DST
        adjacency = edge_tiles[src_index, dst_index].astype(jnp.float32)
        column = blocked[:, dst_index].reshape(col_blocks, TILE, F)
        picked = column[tile_src[src_index, dst_index]].astype(jnp.float32)
        alive_mask = (slot_ids < tile_count[src_index, dst_index]).astype(jnp.float32)
        partial_value = jnp.einsum("tij,tjf->tif", adjacency, picked) * alive_mask[:, None, None]
        summed = jnp.zeros((row_blocks, TILE, F), jnp.float32).at[tile_dst[src_index, dst_index]].add(partial_value)
        rounded = lax.optimization_barrier(summed.astype(jnp.bfloat16)).astype(jnp.float32)
        return aggregate.at[src_index].add(rounded.reshape(N_DST, BLK_DEV, TILE, F)), None

    start_agg = jnp.zeros((N_SRC, N_DST, BLK_DEV, TILE, F), jnp.float32)
    aggregate, _ = lax.scan(forward_step, start_agg, device_ids)
    agg_rows = aggregate.reshape(NODES, F).astype(jnp.bfloat16)
    preact = jnp.dot(agg_rows, weight, preferred_element_type=jnp.float32) + out_bias
    gate_value = jax.nn.sigmoid(preact)
    hidden = (preact * gate_value).astype(jnp.bfloat16)
    pre_grad = out_grad.astype(jnp.float32) * (gate_value * (1.0 + preact * (1.0 - gate_value)))
    pre_grad_b = pre_grad.astype(jnp.bfloat16)
    weight_grad = jnp.dot(agg_rows.T, pre_grad_b, preferred_element_type=jnp.float32)
    bias_grad = jnp.sum(pre_grad, axis=0)
    back = jnp.dot(pre_grad_b, weight.T, preferred_element_type=jnp.float32).astype(jnp.bfloat16)
    grad_rows = back.reshape(N_SRC, row_blocks, TILE, F)

    def backward_step(grad_total, device_index):
        src_index = device_index // N_DST
        dst_index = device_index % N_DST
        adjacency = edge_tiles[src_index, dst_index].astype(jnp.float32)
        wanted = grad_rows[src_index][tile_dst[src_index, dst_index]].astype(jnp.float32)
        alive_mask = (slot_ids < tile_count[src_index, dst_index]).astype(jnp.float32)
        source = jnp.einsum("tji,tjf->tif", adjacency, wanted) * alive_mask[:, None, None]
        summed = jnp.zeros((col_blocks, TILE, F), jnp.float32).at[tile_src[src_index, dst_index]].add(source)
        rounded = lax.optimization_barrier(summed.astype(jnp.bfloat16)).astype(jnp.float32)
        return grad_total.at[:, dst_index].add(rounded.reshape(N_SRC, BLK_DEV, TILE, F)), None

    start_grad = jnp.zeros((N_SRC, N_DST, BLK_DEV, TILE, F), jnp.float32)
    grad_total, _ = lax.scan(backward_step, start_grad, device_ids)
    feature_grad = grad_total.reshape(NODES, F).astype(jnp.bfloat16)
    return (hidden, feature_grad, weight_grad, bias_grad)
```

```python
import jax
import jax.numpy as jnp
from jax import lax
from jax.experimental import pallas as pl
from jax.experimental.pallas import tpu as pltpu
from jax.sharding import PartitionSpec as P


def block_matrix_kernel(blocks, src_ref, dst_ref, count_ref, tiles_ref, out_ref, total):
    size = tiles_ref.shape[1]
    total[...] = jnp.zeros_like(total)

    def add_tile(slot, carry):
        row = pl.multiple_of(dst_ref[slot] // blocks * size, size)
        col = pl.multiple_of(src_ref[slot] * size, size)
        total[pl.ds(row, size), pl.ds(col, size)] += tiles_ref[slot].astype(jnp.float32)
        return carry

    lax.fori_loop(0, count_ref[0], add_tile, 0)
    out_ref[...] = total[...].astype(out_ref.dtype)


def block_matrix(src_ids, dst_ids, tile_total, tiles, blocks, masters, columns):
    size = tiles.shape[1]
    shape = (masters * size, columns * size)
    smem = pl.BlockSpec(memory_space=pltpu.SMEM)
    vmem = pl.BlockSpec(memory_space=pltpu.VMEM)
    held = tiles.size * 2 + shape[0] * shape[1] * 6
    return pl.pallas_call(
        lambda *refs: block_matrix_kernel(blocks, *refs),
        out_shape=jax.ShapeDtypeStruct(shape, jnp.bfloat16),
        in_specs=[smem, smem, smem, vmem],
        out_specs=vmem,
        scratch_shapes=[pltpu.VMEM(shape, jnp.float32)],
        compiler_params=pltpu.CompilerParams(vmem_limit_bytes=held + 4 * 1024 * 1024),
        cost_estimate=pl.CostEstimate(flops=tiles.size, bytes_accessed=held, transcendentals=0),
        name="block_matrix",
    )(src_ids, dst_ids, tile_total, tiles)


def scatter_sum(terms):
    chips = terms.shape[0]
    holders = chips * 2
    me = lax.axis_index("src")
    core = me % 2
    chip = me // 2
    kept = jnp.where(core == 0, terms[:, 0], terms[:, 1])
    given = jnp.where(core == 0, terms[:, 1], terms[:, 0]).astype(jnp.bfloat16)
    got = lax.ppermute(given, "src", [(i, i ^ 1) for i in range(holders)])
    pair = kept + got.astype(jnp.float32)
    result = lax.dynamic_index_in_dim(pair, chip, 0, keepdims=False)
    sent = pair.astype(jnp.bfloat16)
    for step in range(1, chips):
        out = lax.dynamic_index_in_dim(sent, (chip + step) % chips, 0, keepdims=False)
        ring = [(i, (i + 2 * step) % holders) for i in range(holders)]
        result = result + lax.ppermute(out, "src", ring).astype(jnp.float32)
    return result.astype(jnp.bfloat16)


def per_device(features, edge_tiles, tile_src, tile_dst, tile_count, weight, out_bias, out_grad):
    capacity = edge_tiles.shape[2]
    edge_size = edge_tiles.shape[3]
    feat_width = features.shape[1]
    block_rows = features.shape[0]
    blocks = block_rows // edge_size
    masters = lax.axis_size("dst")
    holders = lax.axis_size("src")
    adjacency = edge_tiles.reshape(capacity, edge_size, edge_size)
    src_ids = tile_src.reshape(capacity)
    dst_ids = tile_dst.reshape(capacity)
    tile_total = tile_count.reshape(())
    alive_mask = jnp.arange(capacity, dtype=jnp.int32) < tile_total
    block_ids = jnp.arange(blocks, dtype=jnp.int32)
    owner_ids = dst_ids // blocks
    inner_ids = dst_ids % blocks
    column = lax.all_gather(features, "src", axis=0, tiled=True)
    matrix = block_matrix(
        src_ids, dst_ids, tile_count.reshape(1), adjacency, blocks, masters, holders * blocks
    )
    routing = (owner_ids[None, :] == jnp.arange(masters, dtype=jnp.int32)[:, None]) & alive_mask[
        None, :
    ]
    wanted_block = jnp.max(jnp.where(routing, inner_ids[None, :], 0), axis=1)
    wanted_rows = jnp.broadcast_to(wanted_block[:, None], (masters, edge_size))
    asked = lax.all_to_all(wanted_rows, "dst", split_axis=0, concat_axis=0, tiled=True)
    outgoing = jnp.dot(matrix, column, preferred_element_type=jnp.float32).astype(jnp.bfloat16)
    incoming = lax.all_to_all(
        outgoing.reshape(masters, edge_size, feat_width),
        "dst",
        split_axis=0,
        concat_axis=0,
        tiled=True,
    )
    asked_block = asked[:, 0]
    selector = asked_block[:, None] == block_ids[None, :]
    aggregate = jnp.concatenate(
        [
            jnp.sum(
                jnp.where(selector[:, j, None, None], incoming.astype(jnp.float32), 0.0), axis=0
            ).astype(jnp.bfloat16)
            for j in range(blocks)
        ],
        axis=0,
    )
    preact = jnp.dot(aggregate, weight, preferred_element_type=jnp.float32) + out_bias
    gate_value = jax.nn.sigmoid(preact)
    hidden = (preact * gate_value).astype(jnp.bfloat16)
    pre_grad = out_grad.astype(jnp.float32) * (gate_value * (1.0 + preact * (1.0 - gate_value)))
    pre_grad_b = pre_grad.astype(jnp.bfloat16)
    weight_term = lax.dot_general(
        aggregate, pre_grad_b, (((0,), (0,)), ((), ())), preferred_element_type=jnp.float32
    )
    bias_term = jnp.sum(pre_grad, axis=0, keepdims=True)
    joined = jnp.concatenate(
        [weight_term.astype(jnp.bfloat16), jnp.broadcast_to(bias_term, (16, bias_term.shape[1])).astype(jnp.bfloat16)],
        axis=0,
    )
    reduced = lax.psum(joined, ("src", "dst"))
    weight_grad = reduced[:feat_width].astype(jnp.float32)
    bias_grad = reduced[feat_width].astype(jnp.float32)
    back = lax.dot_general(
        pre_grad_b, weight, (((1,), (1,)), ((), ())), preferred_element_type=jnp.float32
    ).astype(jnp.bfloat16)
    back = back.reshape(blocks, edge_size, feat_width)
    replies = back[0][None]
    for j in range(1, blocks):
        replies = jnp.where(selector[:, j, None, None], back[j][None], replies)
    returned = lax.all_to_all(replies, "dst", split_axis=0, concat_axis=0, tiled=True)
    src_terms = lax.dot_general(
        matrix,
        returned.reshape(masters * edge_size, feat_width),
        (((0,), (0,)), ((), ())),
        preferred_element_type=jnp.float32,
    )
    summed = scatter_sum(src_terms.reshape(holders // 2, 2, block_rows, feat_width))
    return (hidden, summed, weight_grad, bias_grad)


def solution(mesh):
    in_specs = (
        P(("src", "dst"), None),
        P("src", "dst", None, None, None),
        P("src", "dst", None),
        P("src", "dst", None),
        P("src", "dst"),
        P(),
        P(),
        P(("src", "dst"), None),
    )
    out_specs = (P(("src", "dst"), None), P(("src", "dst"), None), P(), P())
    return jax.shard_map(
        per_device, mesh=mesh, in_specs=in_specs, out_specs=out_specs, check_vma=False
    )
```
